32 devices in a mesh: feat: 4 (over y, x), tok: 8 (over z, core).
Axes of the slice: x: 2, y: 2, z: 4, core: 2. Of those that a mesh axis runs over, the one named last changes fastest.
Arguments:
- tokens: bfloat16 [2048, 12288], P('tok', 'feat'), may hold values from -6 to 6
- gate_weight: bfloat16 [16, 5, 768, 768], P('feat', None, 'tok'), may hold values from -0.09375 to 0.09375
- up_weight: bfloat16 [16, 5, 768, 768], P('feat', None, 'tok'), may hold values from -0.09375 to 0.09375
- gate_scale: float32 [16, 5], P('feat'), may hold values from 0.35 to 2.8
- up_scale: float32 [16, 5], P('feat'), may hold values from 0.35 to 2.8
- partners: int32 [16, 5], replicated, may hold values from 0 to 15, as said below
- latent_in: bfloat16 [12288, 768], P('feat'), may hold values from -0.0546875 to 0.0546875
- latent_out: bfloat16 [768, 12288], P(None, 'feat'), may hold values from -0.21875 to 0.21875
Outputs:
- hidden: bfloat16 [2048, 12288], P('tok', 'feat')
- rank_term: bfloat16 [2048, 12288], P('tok', 'feat')
The draws below stay inside these ranges and needn't reach their ends.
Inputs may be any that keep to these rules, and one draw needn't show every extreme that they name: `partners`: row i lists the blocks i, i xor 1, i xor 2, i xor 4 and i xor 8, each once, in some order.
All inputs are finite; a program needn't handle non-finite values.
Results may differ from the reference program's by a relative error of at most 0.015.
Values may be sent and summed in bfloat16 or wider, within the bound.
A program may use at most 128 MiB of HBM per device.

```python
import math
import jax
import jax.numpy as jnp
from jax import lax

BLK = 768
NBLK = 16
PART = 5
RANK = 768
D = 12288
TOKENS = 2048


def draw_partners(key, part):
    row_ids = jnp.arange(NBLK, dtype=jnp.int32)
    offsets = jnp.concatenate([jnp.zeros((1,), jnp.int32), jnp.left_shift(jnp.ones((PART - 1,), jnp.int32), jnp.arange(PART - 1, dtype=jnp.int32))])
    base_ids = jnp.bitwise_xor(row_ids[:, None], offsets[None, :])
    row_keys = jax.random.split(jax.random.fold_in(key, 7), NBLK)
    orders = jax.vmap(lambda row_key: jax.random.permutation(row_key, PART))(row_keys)
    return jnp.take_along_axis(base_ids, orders.astype(jnp.int32), axis=1)


def block_scale(own_key, dims, cuts, least, high):
    factor_of, own = 1.0, jax.random.fold_in(own_key, 6)
    for position, parts in cuts:
        draws = jnp.exp(jax.random.uniform(jax.random.fold_in(own, position), (parts,), jnp.float32, least / len(cuts), high / len(cuts)))
        factor_of = factor_of * jnp.repeat(draws, dims[position] // parts).reshape([-1 if axis == position else 1 for axis in range(len(dims))])
    return factor_of


def centred(rng, shape, deviation, limit, cuts=(), kind=jnp.bfloat16):
    drawn = deviation * jax.random.normal(rng, shape, jnp.float32)
    if cuts:
        drawn = drawn * block_scale(rng, shape, cuts, -0.22, 0.18)
    return jnp.clip(drawn, -limit, limit).astype(kind)


def setup_inputs(seed: int = 0) -> dict:
    key_of = jax.random.split(jax.random.key(seed), 9)
    tokens = centred(key_of[0], (TOKENS, D), 1.0, 6.0, ((0, 8), (1, 4)))
    gate_weight = centred(key_of[1], (NBLK, PART, BLK, BLK), (PART * BLK) ** -0.5, 0.09375, ((0, 4), (2, 8)))
    up_weight = centred(key_of[2], (NBLK, PART, BLK, BLK), (PART * BLK) ** -0.5, 0.09375, ((0, 4), (2, 8)))
    gate_scale = jnp.clip(jnp.exp(math.log(2.8) - 2.0794415 * jax.random.uniform(key_of[3], (NBLK, PART), jnp.float32) ** block_scale(key_of[3], (NBLK, PART), ((0, 4),), -0.2, 0.2)), 0.35, 2.8)
    up_scale = jnp.clip(jnp.exp(math.log(2.8) - 2.0794415 * jax.random.uniform(key_of[4], (NBLK, PART), jnp.float32) ** block_scale(key_of[4], (NBLK, PART), ((0, 4),), -0.2, 0.2)), 0.35, 2.8)
    partners = draw_partners(jax.random.fold_in(key_of[8], 71), 0)
    latent_in = centred(key_of[6], (D, RANK), D ** -0.5, 0.0546875, ((0, 4),))
    latent_out = centred(key_of[7], (RANK, D), RANK ** -0.5, 0.21875, ((1, 4),))
    return dict(tokens=tokens, gate_weight=gate_weight, up_weight=up_weight, gate_scale=gate_scale, up_scale=up_scale, partners=partners, latent_in=latent_in, latent_out=latent_out)


def slot_inputs(tokens, row_ids):
    return jnp.stack([lax.dynamic_slice_in_dim(tokens, (row_ids[slot_idx] * BLK).astype(jnp.int32), BLK, 1) for slot_idx in range(PART)])


def reference(tokens, gate_weight, up_weight, gate_scale, up_scale, partners, latent_in, latent_out):
    def one_block(block_id):
        row_ids = partners[block_id]
        inputs = slot_inputs(tokens, row_ids).astype(jnp.float32)
        gate_terms = jnp.einsum("ktb,kbc->ktc", inputs, gate_weight[block_id].astype(jnp.float32))
        up_terms = jnp.einsum("ktb,kbc->ktc", inputs, up_weight[block_id].astype(jnp.float32))
        gate_sum = jnp.sum(gate_terms * gate_scale[block_id][:, None, None], axis=0)
        up_sum = jnp.sum(up_terms * up_scale[block_id][:, None, None], axis=0)
        return (jax.nn.silu(gate_sum) * up_sum).astype(jnp.bfloat16)

    blocks = lax.map(one_block, jnp.arange(NBLK, dtype=jnp.int32))
    hidden = jnp.transpose(blocks, (1, 0, 2)).reshape(TOKENS, NBLK * BLK)
    latent = jnp.dot(hidden, latent_in, preferred_element_type=jnp.float32).astype(jnp.bfloat16)
    rank_term = jnp.dot(latent, latent_out, preferred_element_type=jnp.float32).astype(jnp.bfloat16)
    return hidden, rank_term
```

```python
import jax
import jax.numpy as jnp
from jax import lax
from jax.sharding import PartitionSpec as P


def swapped(value, axis, bit):
    mask = 2**bit
    pairs = [(source, source ^ mask) for source in range(lax.axis_size(axis))]
    return lax.ppermute(value, axis, pairs)


def per_device(
    tokens, gate_weight, up_weight, gate_scale, up_scale, partners, latent_in, latent_out
):
    tok_rows = tokens.shape[0]
    blocks, slot_count, part_rows, blk_width = gate_weight.shape
    feat_count = lax.axis_size("feat")
    tok_count = lax.axis_size("tok")
    local_bits = blocks.bit_length() - 1
    feat_bits = feat_count.bit_length() - 1

    pieces = tokens.T.reshape(blocks, tok_count, part_rows, tok_rows).transpose(1, 0, 2, 3)
    own = lax.all_to_all(pieces, "tok", 0, 0, tiled=True)
    own = own.transpose(1, 2, 0, 3).reshape(blocks, part_rows, tok_count * tok_rows)
    remote = [swapped(own, "feat", bit_pos) for bit_pos in range(feat_bits)]

    first_block = lax.axis_index("feat") * blocks
    slot_ids = jnp.arange(slot_count, dtype=jnp.int32)
    latent_part = jnp.zeros((tok_rows, latent_in.shape[1]), jnp.float32)
    hidden = []
    for own_block in range(blocks):
        global_id = first_block + own_block
        candidates = [own[own_block]]
        labels = [global_id]
        for bit_pos in range(local_bits + feat_bits):
            if bit_pos < local_bits:
                candidates.append(own[own_block ^ 1 << bit_pos])
            else:
                candidates.append(remote[bit_pos - local_bits][own_block])
            labels.append(jnp.bitwise_xor(global_id, 1 << bit_pos))
        wanted = lax.dynamic_index_in_dim(partners, global_id, 0, keepdims=False)
        matched = wanted[:, None] == jnp.stack(labels)[None, :]
        slot_of = jnp.sum(jnp.where(matched, slot_ids[:, None], 0), axis=0)
        scaled = []
        for weight, scale in ((gate_weight, gate_scale), (up_weight, up_scale)):
            picked = jnp.take(weight[own_block], slot_of, axis=0)
            factor = jnp.take(scale[own_block], slot_of, axis=0)
            scaled.append((picked * factor[:, None, None]).astype(jnp.bfloat16))
        both = jnp.concatenate(scaled, axis=2).reshape(slot_count * part_rows, 2 * blk_width)
        inputs = jnp.concatenate(candidates, axis=0)
        partial = lax.dot_general(
            inputs, both, (((0,), (0,)), ((), ())), preferred_element_type=jnp.float32
        ).astype(jnp.bfloat16)
        sums = lax.psum_scatter(partial, "tok", scatter_dimension=0, tiled=True)
        sums = sums.astype(jnp.float32)
        block_hidden = (jax.nn.silu(sums[:, :blk_width]) * sums[:, blk_width:]).astype(jnp.bfloat16)
        hidden.append(block_hidden)
        rows = latent_in[own_block * blk_width : (own_block + 1) * blk_width]
        latent_part += jnp.dot(block_hidden, rows, preferred_element_type=jnp.float32)
    latent = latent_part
    for bit_pos in range(feat_bits):
        share = latent.astype(jnp.bfloat16)
        latent = share.astype(jnp.float32) + swapped(share, "feat", bit_pos).astype(jnp.float32)
    latent = latent.astype(jnp.bfloat16)
    rank_term = jnp.dot(latent, latent_out, preferred_element_type=jnp.float32).astype(jnp.bfloat16)
    return (jnp.concatenate(hidden, axis=1), rank_term)


def solution(mesh):
    placed = (
        P("tok", "feat"),
        P("feat", None, "tok", None),
        P("feat", None, "tok", None),
        P("feat", None),
        P("feat", None),
        P(),
        P("feat", None),
        P(None, "feat"),
    )
    return jax.shard_map(
        per_device,
        mesh=mesh,
        in_specs=placed,
        out_specs=(P("tok", "feat"), P("tok", "feat")),
        check_vma=False,
    )
```

```python
import jax
import jax.numpy as jnp
from jax import lax
from jax.sharding import PartitionSpec as P


PAIR = 2


def swapped(value, axis, bit):
    mask = 2**bit
    pairs = [(source, source ^ mask) for source in range(lax.axis_size(axis))]
    return lax.ppermute(value, axis, pairs)


def moved(value, chip_pairs):
    pairs = [
        (PAIR * source + lane, PAIR * target + lane)
        for source, target in chip_pairs
        for lane in range(PAIR)
    ]
    return lax.ppermute(value, "tok", pairs)


def after(value, *others):
    return lax.optimization_barrier((value, *others))[0]


def per_device(
    tokens, gate_weight, up_weight, gate_scale, up_scale, partners, latent_in, latent_out
):
    tok_rows = tokens.shape[0]
    blocks, slot_count, part_rows, blk_width = gate_weight.shape
    feat_count = lax.axis_size("feat")
    chips = lax.axis_size("tok") // PAIR
    half = chips // 2
    local_bits = blocks.bit_length() - 1
    feat_bits = feat_count.bit_length() - 1
    place = lax.axis_index("tok")
    chip, lane = place // PAIR, place % PAIR
    on_right = chip >= half
    distance = jnp.where(on_right, chip - half, half - 1 - chip)
    inward = [[(half - 1 - q, half - 1), (half + q, half)] for q in range(half)]
    across = [[(half - 1 - q, half), (half + q, half - 1)] for q in range(half)]
    outward = [[(half - 1, half - 1 - q), (half, half + q)] for q in range(half)]

    first_block = lax.axis_index("feat") * blocks
    slot_ids = jnp.arange(slot_count, dtype=jnp.int32)
    ready = []
    for own_block in range(blocks):
        global_id = first_block + own_block
        labels = [global_id]
        for bit_pos in range(local_bits + feat_bits):
            labels.append(jnp.bitwise_xor(global_id, 1 << bit_pos))
        wanted = lax.dynamic_index_in_dim(partners, global_id, 0, keepdims=False)
        matched = wanted[:, None] == jnp.stack(labels)[None, :]
        slot_of = jnp.sum(jnp.where(matched, slot_ids[:, None], 0), axis=0)
        scaled = []
        for weight, scale in ((gate_weight, gate_scale), (up_weight, up_scale)):
            picked = jnp.take(weight[own_block], slot_of, axis=0)
            factor = jnp.take(scale[own_block], slot_of, axis=0)
            scaled.append((picked * factor[:, None, None]).astype(jnp.bfloat16))
        ready.append(jnp.concatenate(scaled, axis=2))

    pieces = tokens.T.reshape(blocks, chips, PAIR, part_rows, tok_rows).transpose(2, 1, 0, 3, 4)
    pieces = jnp.where(lane == 0, pieces, pieces[::-1])
    left, right = pieces[:, :half][:, ::-1], pieces[:, half:]
    near = jnp.where(on_right, right, left)
    far = jnp.where(on_right, left, right)
    from_far = [moved(far, across[q]) for q in range(half)]
    chain = from_far[-1]
    shipped = []

    def ship(block, chain):
        parts = [ready[block]]
        for q in range(1, half):
            parts.append(moved(after(ready[block], chain), inward[q]))
            chain = parts[-1]
        shipped.append(parts)
        return chain

    def bits_of(value, chain):
        value_in = after(value, chain) if chain is not None else value
        return [swapped(value_in, "feat", bit_pos) for bit_pos in range(feat_bits)]

    chain = ship(0, chain)
    far_remote = [bits_of(value, None) for value in from_far]
    for own_block in range(1, min(2, blocks)):
        chain = ship(own_block, chain)
    from_near = [near]
    for q in range(1, half):
        from_near.append(moved(after(near, chain), inward[q]))
        chain = from_near[-1]
    near_remote = [bits_of(value, far_remote[-1][-1]) for value in from_near]
    for own_block in range(2, blocks):
        chain = ship(own_block, chain)

    def inputs_of(own_block, groups, remotes):
        rows = []
        for group, remote in zip(groups, remotes):
            picked = [group[:, :, own_block]]
            for bit_pos in range(local_bits):
                picked.append(group[:, :, own_block ^ 1 << bit_pos])
            for bit_pos in range(feat_bits):
                picked.append(remote[bit_pos][:, :, own_block])
            rows.append(jnp.stack(picked, axis=2).reshape(-1, tok_rows))
        return jnp.concatenate(rows, axis=1)

    def product(inputs, weights):
        return lax.dot_general(
            inputs, weights, (((0,), (0,)), ((), ())), preferred_element_type=jnp.float32
        )

    latent_part = jnp.zeros((tok_rows, latent_in.shape[1]), jnp.float32)
    hidden = []
    for own_block in range(blocks):
        mine = jnp.concatenate(shipped[own_block], axis=0)
        other = swapped(mine, "tok", 0)
        weights = jnp.concatenate([mine, other], axis=0).reshape(-1, 2 * blk_width)
        away = product(inputs_of(own_block, from_far, far_remote), weights).astype(jnp.bfloat16)
        back = moved(away, across[0])
        home = product(inputs_of(own_block, from_near, near_remote), weights)
        sums = home + back.astype(jnp.float32)
        done = (jax.nn.silu(sums[:, :blk_width]) * sums[:, blk_width:]).astype(jnp.bfloat16)
        block_hidden = done[:tok_rows]
        for q in range(1, half):
            sent = moved(done[q * tok_rows : (q + 1) * tok_rows], outward[q])
            block_hidden = jnp.where(distance == q, sent, block_hidden)
        hidden.append(block_hidden)
        rows = latent_in[own_block * blk_width : (own_block + 1) * blk_width]
        latent_part += jnp.dot(block_hidden, rows, preferred_element_type=jnp.float32)
    latent = latent_part
    for bit_pos in range(feat_bits):
        share = latent.astype(jnp.bfloat16)
        latent = share.astype(jnp.float32) + swapped(share, "feat", bit_pos).astype(jnp.float32)
    latent = latent.astype(jnp.bfloat16)
    rank_term = jnp.dot(latent, latent_out, preferred_element_type=jnp.float32).astype(jnp.bfloat16)
    return (jnp.concatenate(hidden, axis=1), rank_term)


def solution(mesh):
    placed = (
        P("tok", "feat"),
        P("feat", None, "tok", None),
        P("feat", None, "tok", None),
        P("feat", None),
        P("feat", None),
        P(),
        P("feat", None),
        P(None, "feat"),
    )
    return jax.shard_map(
        per_device,
        mesh=mesh,
        in_specs=placed,
        out_specs=(P("tok", "feat"), P("tok", "feat")),
        check_vma=False,
    )
```
